32 devices in a mesh: books: 2 (over x), wide: 4 (over y, core), narrow: 4 (over z).
Axes of the slice: x: 2, y: 2, z: 4, core: 2. Of those that a mesh axis runs over, the one named last changes fastest.
Arguments:
- dec_queries: bfloat16 [16384, 1024], P(('books', 'wide', 'narrow')), parts along dimension 0, may hold values from -6 to 6
- dec_keys: bfloat16 [16384, 1024], P(('books', 'wide', 'narrow')), parts along dimension 0, may hold values from -6 to 6
- dec_values: bfloat16 [16384, 1024], P(('books', 'wide', 'narrow')), parts along dimension 0, may hold values from -6 to 6
- enc_keys: bfloat16 [16384, 1024], P(('books', 'wide', 'narrow')), parts along dimension 0, may hold values from -6 to 6
- enc_values: bfloat16 [16384, 1024], P(('books', 'wide', 'narrow')), parts along dimension 0, may hold values from -6 to 6
- out_weight: bfloat16 [1024, 2048], replicated, may hold values from -0.1875 to 0.1875
- head_gain: float32 [1024], replicated, may hold values from 0.1 to 1.9
Outputs:
- output: bfloat16 [16384, 2048], P(('books', 'wide', 'narrow')), parts along dimension 0
The draws below stay inside these ranges and needn't reach their ends.
There are 2 independent parts, one for each index of `books`. The reference program is written for one: setup_inputs(seed, part) draws one part's arguments, and reference() takes and returns one part's arrays. A program takes and returns all parts, laid end to end along the dimension named above; an argument that names none is the same for every part. Nothing has to cross between parts.
All inputs are finite; a program needn't handle non-finite values.
Results may differ from the reference program's by a relative error of at most 0.0058.
Values sent between devices are 32-bit elements; how exact they have to be, the bound alone decides.
A program may use at most 128 MiB of HBM per device.

```python
import jax
import jax.numpy as jnp
from jax import lax

D = 2048
HEADS = 8
HEAD_DIM = 128
BLOCK = 128
TOKENS = 8192


def steps_of(key, extent, shards, smallest, largest):
    def one(axis_at, blocks):
        steps = jax.random.uniform(jax.random.fold_in(jax.random.fold_in(key, 6), axis_at), (blocks,), jnp.float32, smallest / len(shards), largest / len(shards))
        return jnp.repeat(jnp.exp(steps), extent[axis_at] // blocks).reshape((-1,) + (1,) * (len(extent) - axis_at - 1))

    loudness = one(*shards[0])
    for cut in shards[1:]:
        loudness = loudness * one(*cut)
    return loudness


def normal_values(stream_key, extent, scale, reach, cuts=(), kind=jnp.bfloat16):
    loudness = steps_of(stream_key, extent, cuts, -0.22, 0.18) if cuts else 1.0
    values = jax.random.normal(stream_key, extent, jnp.float32) * scale * loudness
    return jnp.minimum(jnp.maximum(values, -reach), reach).astype(kind)


def setup_inputs(seed: int = 0, part: int = 0) -> dict:
    seeds = jax.random.split(jax.random.key(seed), 8)
    part_keys = jax.random.split(jax.random.fold_in(seeds[7], part), 8)
    dec_queries = normal_values(part_keys[0], (TOKENS, HEADS * HEAD_DIM), 1.0, 6.0, ((0, 16),))
    dec_keys = normal_values(part_keys[1], (TOKENS, HEADS * HEAD_DIM), 1.0, 6.0, ((0, 16),))
    dec_values = normal_values(part_keys[2], (TOKENS, HEADS * HEAD_DIM), 1.0, 6.0, ((0, 16),))
    enc_keys = normal_values(part_keys[3], (TOKENS, HEADS * HEAD_DIM), 1.0, 6.0, ((0, 16),))
    enc_values = normal_values(part_keys[4], (TOKENS, HEADS * HEAD_DIM), 1.0, 6.0, ((0, 16),))
    out_weight = normal_values(seeds[5], (HEADS * HEAD_DIM, D), (HEADS * HEAD_DIM) ** -0.5, 0.1875)
    head_gain = jnp.clip(1.0 + 0.18 * jax.random.normal(seeds[6], (HEADS * HEAD_DIM,), jnp.float32), 0.1, 1.9)
    return {"dec_queries": dec_queries, "dec_keys": dec_keys, "dec_values": dec_values, "enc_keys": enc_keys, "enc_values": enc_values, "out_weight": out_weight, "head_gain": head_gain}


def reference(dec_queries, dec_keys, dec_values, enc_keys, enc_values, out_weight, head_gain):
    total = dec_queries.shape[0]
    block_count = total // BLOCK
    enc_key32 = enc_keys.astype(jnp.float32).reshape(total, HEADS, HEAD_DIM)
    enc_val32 = enc_values.astype(jnp.float32).reshape(total, HEADS, HEAD_DIM)
    memory = jnp.einsum('thd,the->hde', enc_key32, enc_val32)
    gain = head_gain.astype(jnp.float32).reshape(HEADS, HEAD_DIM)
    rows = lax.broadcasted_iota(jnp.int32, (BLOCK, BLOCK), 0)
    columns = lax.broadcasted_iota(jnp.int32, (BLOCK, BLOCK), 1)
    causal = rows >= columns

    def advance(carry, block):
        query_blk, key_blk, value_blk = block
        query32 = query_blk.astype(jnp.float32).reshape(BLOCK, HEADS, HEAD_DIM)
        key32 = key_blk.astype(jnp.float32).reshape(BLOCK, HEADS, HEAD_DIM)
        value32 = value_blk.astype(jnp.float32).reshape(BLOCK, HEADS, HEAD_DIM)
        scores = jnp.einsum('chd,shd->hcs', query32, key32)
        scores = jnp.where(causal[None], scores, jnp.zeros_like(scores))
        scores_bf = lax.optimization_barrier(scores.astype(jnp.bfloat16)).astype(jnp.float32)
        within_block = jnp.einsum('hcs,she->che', scores_bf, value32)
        carry_bf = lax.optimization_barrier(carry.astype(jnp.bfloat16)).astype(jnp.float32)
        from_state = jnp.einsum('chd,hde->che', query32, carry_bf)
        attended = within_block + from_state
        inverse = lax.rsqrt(lax.optimization_barrier(jnp.mean(attended * attended, axis=-1, keepdims=True)) + 1e-06)
        normed = (attended * inverse * gain[None]).astype(jnp.bfloat16).reshape(BLOCK, HEADS * HEAD_DIM)
        result = jnp.dot(normed, out_weight, preferred_element_type=jnp.float32).astype(jnp.bfloat16)
        new_carry = carry + jnp.einsum('chd,che->hde', key32, value32)
        return (new_carry, result)
    blocked = (dec_queries.reshape(block_count, BLOCK, HEADS * HEAD_DIM), dec_keys.reshape(block_count, BLOCK, HEADS * HEAD_DIM), dec_values.reshape(block_count, BLOCK, HEADS * HEAD_DIM))
    final_state, results = lax.scan(advance, memory, blocked)
    return results.reshape(total, D)
```

```python
import functools

import jax
import jax.numpy as jnp
from jax import lax
from jax.experimental import pallas as pl
from jax.experimental.pallas import tpu as pltpu
from jax.sharding import PartitionSpec as P

HEADS = 8
HEAD_DIM = 128
BLOCK = 128
WIDE_LAG = 1
NARROW_LAG = 2
MESH = pl.DeviceIdType.MESH


def dot(a, b, contract):
    return lax.dot_general(a, b, (contract, ((), ())), preferred_element_type=jnp.float32)


def kernel(
    wide, narrow,
    q_hbm, dk_hbm, dv_hbm, ek_hbm, ev_hbm, gain_ref, out_ref,
    q, dk, dv, ek, ev, scores, enc, cum, base,
    f_out, g_out, p_out, r_out, f_in, g_in, p_in, r_in,
    load_sem, send_sem, recv_sem,
):
    w = lax.axis_index("wide")
    z = lax.axis_index("narrow")
    tokens = q.shape[1]
    blocks = tokens // BLOCK
    span = 2 * BLOCK if blocks % 2 == 0 else BLOCK

    def load(i, h):
        src, dst = ((ek_hbm, ek), (ev_hbm, ev), (dk_hbm, dk), (dv_hbm, dv), (q_hbm, q))[i]
        columns = pl.ds(pl.multiple_of(h * HEAD_DIM, HEAD_DIM), HEAD_DIM)
        return pltpu.make_async_copy(src.at[:, columns], dst.at[h], load_sem.at[i, h])

    barrier = pltpu.get_barrier_semaphore()
    has = (w > 0, w < wide - 1, z > 0, z < narrow - 1)
    peers = ({"wide": w - 1}, {"wide": w + 1}, {"narrow": z - 1}, {"narrow": z + 1})
    for there, peer in zip(has, peers):

        @pl.when(there)
        def _():
            pl.semaphore_signal(barrier, inc=1, device_id=peer, device_id_type=MESH)

    for h in range(HEADS):
        for i in range(4):
            load(i, h).start()
    for h in range(HEADS):
        load(4, h).start()

    for there, ref in zip(has, (f_in, g_in, p_in, r_in)):

        @pl.when(jnp.logical_not(there))
        def _():
            ref[...] = jnp.zeros_like(ref)

    pl.semaphore_wait(barrier, sum(there.astype(jnp.int32) for there in has))

    chains = (
        (f_out, f_in, 0, 1),
        (g_out, g_in, 1, 0),
        (p_out, p_in, 2, 3),
        (r_out, r_in, 3, 2),
    )

    def remote(c, h):
        out, into, _, to = chains[c]
        return pltpu.make_async_remote_copy(
            src_ref=out.at[h],
            dst_ref=into.at[h],
            send_sem=send_sem.at[c, h],
            recv_sem=recv_sem.at[c, h],
            device_id=peers[to],
            device_id_type=MESH,
        )

    def inside(h):
        return jnp.logical_and(h >= 0, h < HEADS)

    def link(c, h, value):
        out, into, source, to = chains[c]

        @pl.when(inside(h))
        def _():
            @pl.when(has[source])
            def _():
                remote(c, h).wait_recv()

            @pl.when(has[to])
            def _():
                out[h] = into[h] + value(h)
                remote(c, h).start()

    def states(h):
        for i in range(4):
            load(i, h).wait()
        enc[h] = dot(ek[h], ev[h], ((0,), (0,)))
        total = None
        for b in range(blocks):
            rows = pl.ds(b * BLOCK, BLOCK)
            part = dot(dk[h, rows, :], dv[h, rows, :], ((0,), (0,)))
            total = part if total is None else total + part
            cum[h, b] = total

    def make_scores(h):
        load(4, h).wait()
        rows = lax.broadcasted_iota(jnp.int32, (span, span), 0)
        columns = lax.broadcasted_iota(jnp.int32, (span, span), 1)
        keep = jnp.logical_and(rows >= columns, rows // BLOCK == columns // BLOCK)
        for s in range(tokens // span):
            part = pl.ds(s * span, span)
            block = dot(q[h, part, :], dk[h, part, :], ((1,), (1,)))
            block = jnp.where(keep, block, 0.0).astype(jnp.bfloat16)
            for i in range(span // BLOCK):
                near = slice(i * BLOCK, (i + 1) * BLOCK)
                scores[h, pl.ds(s * span + i * BLOCK, BLOCK), :] = block[near, near]

    def finish(h):
        carry = base[h] + p_in[h] + r_in[h]
        columns = pl.ds(pl.multiple_of(h * HEAD_DIM, HEAD_DIM), HEAD_DIM)
        gain = gain_ref[pl.ds(h, 1), :]
        for b in range(blocks):
            rows = pl.ds(b * BLOCK, BLOCK)
            state = carry if b == 0 else carry + cum[h, b - 1]
            left = jnp.concatenate([scores[h, rows, :], q[h, rows, :]], axis=1)
            right = jnp.concatenate([dv[h, rows, :], state.astype(jnp.bfloat16)], axis=0)
            attended = dot(left, right, ((1,), (0,)))
            inverse = lax.rsqrt(jnp.mean(attended * attended, axis=-1, keepdims=True) + 1e-06)
            out_ref[rows, columns] = (attended * inverse * gain).astype(jnp.bfloat16)

    def total(h):
        return cum[h, blocks - 1]

    ready = WIDE_LAG * jnp.maximum(w, wide - 1 - w)
    last = ready + NARROW_LAG * jnp.maximum(z, narrow - 1 - z)

    def slot(t, _):
        @pl.when(t < HEADS)
        def _():
            states(t)

        link(0, t - WIDE_LAG * w, lambda h: enc[h] + total(h))
        link(1, t - WIDE_LAG * (wide - 1 - w), lambda h: enc[h])

        @pl.when(inside(t - ready))
        def _():
            h = t - ready
            base[h] = enc[h] + f_in[h] + g_in[h]

        link(2, t - ready - NARROW_LAG * z, lambda h: base[h] + total(h))
        link(3, t - ready - NARROW_LAG * (narrow - 1 - z), lambda h: base[h])

        @pl.when(t < HEADS)
        def _():
            make_scores(t)

        @pl.when(inside(t - last))
        def _():
            finish(t - last)

        return 0

    slots = HEADS + WIDE_LAG * (wide - 1) + NARROW_LAG * (narrow - 1)
    lax.fori_loop(0, slots, slot, 0)

    for c in range(4):

        @pl.when(has[chains[c][3]])
        def _():
            for h in range(HEADS):
                remote(c, h).wait_send()


def local(wide, narrow, dec_queries, dec_keys, dec_values, enc_keys, enc_values, out_weight, head_gain):
    tokens = dec_queries.shape[0]
    blocks = tokens // BLOCK
    heads_in = pltpu.VMEM((HEADS, tokens, HEAD_DIM), jnp.bfloat16)
    state = pltpu.VMEM((HEADS, HEAD_DIM, HEAD_DIM), jnp.float32)
    normed = pl.pallas_call(
        functools.partial(kernel, wide, narrow),
        out_shape=jax.ShapeDtypeStruct((tokens, HEADS * HEAD_DIM), jnp.bfloat16),
        in_specs=[pl.BlockSpec(memory_space=pl.ANY)] * 5 + [pl.BlockSpec(memory_space=pltpu.VMEM)],
        out_specs=pl.BlockSpec(memory_space=pltpu.VMEM),
        scratch_shapes=[heads_in] * 5
        + [pltpu.VMEM((HEADS, tokens, BLOCK), jnp.bfloat16), state]
        + [pltpu.VMEM((HEADS, blocks, HEAD_DIM, HEAD_DIM), jnp.float32), state]
        + [state] * 8
        + [
            pltpu.SemaphoreType.DMA((5, HEADS)),
            pltpu.SemaphoreType.DMA((4, HEADS)),
            pltpu.SemaphoreType.DMA((4, HEADS)),
        ],
        compiler_params=pltpu.CompilerParams(
            collective_id=0, has_side_effects=True, vmem_limit_bytes=40 * 1024 * 1024
        ),
        cost_estimate=pl.CostEstimate(
            flops=5 * 2 * tokens * HEADS * HEAD_DIM * HEAD_DIM,
            bytes_accessed=6 * 2 * tokens * HEADS * HEAD_DIM,
            transcendentals=0,
        ),
    )(dec_queries, dec_keys, dec_values, enc_keys, enc_values, head_gain.reshape(HEADS, HEAD_DIM))
    return jnp.dot(normed, out_weight, preferred_element_type=jnp.float32).astype(jnp.bfloat16)


def solution(mesh):
    tokens = P(("books", "wide", "narrow"), None)
    return jax.shard_map(
        functools.partial(local, mesh.shape["wide"], mesh.shape["narrow"]),
        mesh=mesh,
        in_specs=(tokens,) * 5 + (P(), P()),
        out_specs=tokens,
        check_vma=False,
    )
```

```python
import functools

import jax
import jax.numpy as jnp
from jax import lax
from jax.experimental import pallas as pl
from jax.experimental.pallas import tpu as pltpu
from jax.sharding import PartitionSpec as P

HEADS = 8
HEAD_DIM = 128
BLOCK = 128
PIECES = 2
ROWS = HEAD_DIM // PIECES
CHUNKS = HEADS * PIECES
GROUP = 2
GROUPS = HEADS // GROUP
WIDE_LAG = 4
NARROW_LAG = 5
PROJECT_TILE = 512
MESH = pl.DeviceIdType.MESH


def dot(a, b, contract):
    return lax.dot_general(a, b, (contract, ((), ())), preferred_element_type=jnp.float32)


def kernel(
    wide, narrow,
    q_hbm, dk_hbm, dv_hbm, ek_hbm, ev_hbm, weight_hbm, gain_hbm, out_ref,
    q, dk, dv, ek, ev, weight, gain, scores, normed, acc, enc, total, cum, base,
    f_out, g_out, p_out, r_out, f_in, g_in, p_in, r_in,
    load_sem, weight_sem, gain_sem, send_sem, recv_sem,
):
    w = lax.axis_index("wide")
    z = lax.axis_index("narrow")
    tokens = q.shape[1]
    blocks = tokens // BLOCK
    span = 2 * BLOCK if blocks % 2 == 0 else BLOCK
    group = GROUP * HEAD_DIM

    def load(i, h):
        src, dst = ((ek_hbm, ek), (ev_hbm, ev), (dk_hbm, dk), (dv_hbm, dv), (q_hbm, q))[i]
        columns = pl.ds(pl.multiple_of(h * HEAD_DIM, HEAD_DIM), HEAD_DIM)
        return pltpu.make_async_copy(src.at[:, columns], dst.at[h], load_sem.at[i, h])

    def load_weight(g):
        rows = pl.ds(pl.multiple_of(g * group, group), group)
        return pltpu.make_async_copy(weight_hbm.at[rows, :], weight.at[rows, :], weight_sem.at[g])

    load_gain = pltpu.make_async_copy(gain_hbm, gain, gain_sem)

    def fetch(h):
        for i in range(5):
            load(i, h).start()

    def states(h):
        for i in range(4):
            load(i, h).wait()
        pieces = pl.ds(h * PIECES, PIECES)
        enc[pieces] = dot(ek[h], ev[h], ((0,), (0,))).reshape(PIECES, ROWS, HEAD_DIM)
        so_far = None
        for b in range(blocks):
            rows = pl.ds(b * BLOCK, BLOCK)
            part = dot(dk[h, rows, :], dv[h, rows, :], ((0,), (0,)))
            so_far = part if so_far is None else so_far + part
            if b < blocks - 1:
                cum[h, b] = so_far
        total[pieces] = so_far.reshape(PIECES, ROWS, HEAD_DIM)

    barrier = pltpu.get_barrier_semaphore()
    has = (w > 0, w < wide - 1, z > 0, z < narrow - 1)
    peers = ({"wide": w - 1}, {"wide": w + 1}, {"narrow": z - 1}, {"narrow": z + 1})
    fetch(0)
    for there, peer in zip(has, peers):

        @pl.when(there)
        def _():
            pl.semaphore_signal(barrier, inc=1, device_id=peer, device_id_type=MESH)

    fetch(1)
    fetch(2)
    load_gain.start()

    for there, ref in zip(has, (f_in, g_in, p_in, r_in)):

        @pl.when(jnp.logical_not(there))
        def _():
            ref[...] = jnp.zeros_like(ref)

    states(0)
    load_gain.wait()
    pl.semaphore_wait(barrier, sum(there.astype(jnp.int32) for there in has))

    chains = (
        (f_out, f_in, 0, 1),
        (g_out, g_in, 1, 0),
        (p_out, p_in, 2, 3),
        (r_out, r_in, 3, 2),
    )

    def remote(c, n):
        out, into, _, to = chains[c]
        return pltpu.make_async_remote_copy(
            src_ref=out.at[n],
            dst_ref=into.at[n],
            send_sem=send_sem.at[c, n],
            recv_sem=recv_sem.at[c, n],
            device_id=peers[to],
            device_id_type=MESH,
        )

    def inside(n):
        return jnp.logical_and(n >= 0, n < CHUNKS)

    def link(c, n, value):
        out, into, source, to = chains[c]

        @pl.when(inside(n))
        def _():
            @pl.when(has[source])
            def _():
                remote(c, n).wait_recv()

            @pl.when(has[to])
            def _():
                out[n] = into[n] + value(n)
                remote(c, n).start()

    def make_scores(h):
        load(4, h).wait()
        rows = lax.broadcasted_iota(jnp.int32, (span, span), 0)
        columns = lax.broadcasted_iota(jnp.int32, (span, span), 1)
        keep = jnp.logical_and(rows >= columns, rows // BLOCK == columns // BLOCK)
        for s in range(tokens // span):
            part = pl.ds(s * span, span)
            block = dot(q[h, part, :], dk[h, part, :], ((1,), (1,)))
            block = jnp.where(keep, block, 0.0).astype(jnp.bfloat16)
            for i in range(span // BLOCK):
                near = slice(i * BLOCK, (i + 1) * BLOCK)
                scores[h, pl.ds(s * span + i * BLOCK, BLOCK), :] = block[near, near]

    def finish(h):
        pieces = pl.ds(h * PIECES, PIECES)
        carry = (base[pieces] + p_in[pieces] + r_in[pieces]).reshape(HEAD_DIM, HEAD_DIM)
        columns = pl.ds(pl.multiple_of(h * HEAD_DIM, HEAD_DIM), HEAD_DIM)
        for b in range(blocks):
            rows = pl.ds(b * BLOCK, BLOCK)
            state = carry if b == 0 else carry + cum[h, b - 1]
            left = jnp.concatenate([scores[h, rows, :], q[h, rows, :]], axis=1)
            right = jnp.concatenate([dv[h, rows, :], state.astype(jnp.bfloat16)], axis=0)
            attended = dot(left, right, ((1,), (0,)))
            inverse = lax.rsqrt(jnp.mean(attended * attended, axis=-1, keepdims=True) + 1e-06)
            normed[rows, columns] = (attended * inverse * gain[pl.ds(h, 1), :]).astype(jnp.bfloat16)

    def project(g):
        depth = pl.ds(pl.multiple_of(g * group, group), group)
        load_weight(g).wait()
        tile = min(PROJECT_TILE, out_ref.shape[1])

        def over(store):
            for j in range(out_ref.shape[1] // tile):
                columns = slice(j * tile, (j + 1) * tile)
                store(columns, dot(normed[:, depth], weight[depth, columns], ((1,), (0,))))

        @pl.when(g == 0)
        def _():
            def store(columns, value):
                acc[:, columns] = value

            over(store)

        @pl.when(jnp.logical_and(g > 0, g < GROUPS - 1))
        def _():
            def store(columns, value):
                acc[:, columns] += value

            over(store)

        @pl.when(g == GROUPS - 1)
        def _():
            def store(columns, value):
                out_ref[:, columns] = (acc[:, columns] + value).astype(jnp.bfloat16)

            over(store)

    ready = WIDE_LAG * jnp.maximum(w, wide - 1 - w)
    last = ready + NARROW_LAG * jnp.maximum(z, narrow - 1 - z)

    def slot(t, _):
        h = t // PIECES
        live = jnp.logical_and(h < HEADS, t % PIECES == 0)

        @pl.when(jnp.logical_and(live, h > 0))
        def _():
            states(h)

        link(0, t - WIDE_LAG * w, lambda n: enc[n] + total[n])
        link(1, t - WIDE_LAG * (wide - 1 - w), lambda n: enc[n])

        @pl.when(inside(t - ready))
        def _():
            n = t - ready
            base[n] = enc[n] + f_in[n] + g_in[n]

        link(2, t - ready - NARROW_LAG * z, lambda n: base[n] + total[n])
        link(3, t - ready - NARROW_LAG * (narrow - 1 - z), lambda n: base[n])

        @pl.when(live)
        def _():
            @pl.when(h + 3 < HEADS)
            def _():
                fetch(h + 3)

        after = t - (PIECES - 1)

        @pl.when(jnp.logical_and(after >= 0, jnp.logical_and(after // PIECES < HEADS, after % PIECES == 0)))
        def _():
            make_scores(after // PIECES)

        early = t // (GROUP * PIECES)

        @pl.when(jnp.logical_and(early < GROUPS, t % (GROUP * PIECES) == 0))
        def _():
            load_weight(early).start()

        n = t - last
        done = n - (PIECES - 1)

        @pl.when(jnp.logical_and(done >= 0, jnp.logical_and(done // PIECES < HEADS, done % PIECES == 0)))
        def _():
            finish(done // PIECES)

        whole = n - (GROUP * PIECES - 1)

        @pl.when(
            jnp.logical_and(
                whole >= 0, jnp.logical_and(whole < CHUNKS, whole % (GROUP * PIECES) == 0)
            )
        )
        def _():
            project(whole // (GROUP * PIECES))

        return 0

    slots = CHUNKS + WIDE_LAG * (wide - 1) + NARROW_LAG * (narrow - 1)
    lax.fori_loop(0, slots, slot, 0)

    for c in range(4):

        @pl.when(has[chains[c][3]])
        def _():
            for n in range(CHUNKS):
                remote(c, n).wait_send()


def local(wide, narrow, dec_queries, dec_keys, dec_values, enc_keys, enc_values, out_weight, head_gain):
    tokens = dec_queries.shape[0]
    blocks = tokens // BLOCK
    depth, model = out_weight.shape
    heads_in = pltpu.VMEM((HEADS, tokens, HEAD_DIM), jnp.bfloat16)
    state = pltpu.VMEM((CHUNKS, ROWS, HEAD_DIM), jnp.float32)
    held = [
        pltpu.with_memory_space_constraint(x, pltpu.HBM)
        for x in (dec_queries, dec_keys, dec_values, enc_keys, enc_values, out_weight)
    ]
    gain = pltpu.with_memory_space_constraint(head_gain.reshape(HEADS, HEAD_DIM), pltpu.HBM)
    return pl.pallas_call(
        functools.partial(kernel, wide, narrow),
        out_shape=jax.ShapeDtypeStruct((tokens, model), jnp.bfloat16),
        in_specs=[pl.BlockSpec(memory_space=pltpu.HBM)] * 7,
        out_specs=pl.BlockSpec(memory_space=pltpu.VMEM),
        scratch_shapes=[heads_in] * 5
        + [
            pltpu.VMEM((depth, model), jnp.bfloat16),
            pltpu.VMEM((HEADS, HEAD_DIM), jnp.float32),
            pltpu.VMEM((HEADS, tokens, BLOCK), jnp.bfloat16),
            pltpu.VMEM((tokens, depth), jnp.bfloat16),
            pltpu.VMEM((tokens, model), jnp.float32),
            state,
            state,
            pltpu.VMEM((HEADS, max(blocks - 1, 1), HEAD_DIM, HEAD_DIM), jnp.float32),
            state,
        ]
        + [state] * 8
        + [
            pltpu.SemaphoreType.DMA((5, HEADS)),
            pltpu.SemaphoreType.DMA((GROUPS,)),
            pltpu.SemaphoreType.DMA,
            pltpu.SemaphoreType.DMA((4, CHUNKS)),
            pltpu.SemaphoreType.DMA((4, CHUNKS)),
        ],
        compiler_params=pltpu.CompilerParams(
            collective_id=0, has_side_effects=True, vmem_limit_bytes=48 * 1024 * 1024
        ),
    )(*held, gain)


def solution(mesh):
    tokens = P(("books", "wide", "narrow"), None)
    return jax.shard_map(
        functools.partial(local, mesh.shape["wide"], mesh.shape["narrow"]),
        mesh=mesh,
        in_specs=(tokens,) * 5 + (P(), P()),
        out_specs=tokens,
        check_vma=False,
    )
```

```python
import functools

import jax
import jax.numpy as jnp
from jax import lax
from jax.experimental import pallas as pl
from jax.experimental.pallas import tpu as pltpu
from jax.sharding import PartitionSpec as P

HEADS = 8
HEAD_DIM = 128
BLOCK = 128
PIECES = 1
ROWS = HEAD_DIM // PIECES
CHUNKS = HEADS * PIECES
GROUP = 2
GROUPS = HEADS // GROUP
WIDE_LAG = 2
NARROW_LAG = 3
PROJECT_TILE = 512
SCORES_AHEAD = 3
MESH = pl.DeviceIdType.MESH


def dot(a, b, contract):
    return lax.dot_general(a, b, (contract, ((), ())), preferred_element_type=jnp.float32)


def kernel(
    wide, narrow,
    q_hbm, dk_hbm, dv_hbm, ek_hbm, ev_hbm, weight_hbm, gain_hbm, out_ref,
    q, dk, dv, ek, ev, weight, gain, scores, normed, acc, enc, total, cum, base,
    f_out, g_out, p_out, r_out, f_in, g_in, p_in, r_in,
    load_sem, weight_sem, gain_sem, send_sem, recv_sem,
):
    w = lax.axis_index("wide")
    z = lax.axis_index("narrow")
    tokens = q.shape[1]
    blocks = tokens // BLOCK
    span = 2 * BLOCK if blocks % 2 == 0 else BLOCK
    group = GROUP * HEAD_DIM

    def load(i, h):
        src, dst = ((ek_hbm, ek), (ev_hbm, ev), (dk_hbm, dk), (dv_hbm, dv), (q_hbm, q))[i]
        columns = pl.ds(pl.multiple_of(h * HEAD_DIM, HEAD_DIM), HEAD_DIM)
        return pltpu.make_async_copy(src.at[:, columns], dst.at[h], load_sem.at[i, h])

    def load_weight(g):
        rows = pl.ds(pl.multiple_of(g * group, group), group)
        return pltpu.make_async_copy(weight_hbm.at[rows, :], weight.at[rows, :], weight_sem.at[g])

    load_gain = pltpu.make_async_copy(gain_hbm, gain, gain_sem)

    def fetch(h):
        for i in range(5):
            load(i, h).start()

    def states(h):
        for i in range(4):
            load(i, h).wait()
        pieces = pl.ds(h * PIECES, PIECES)
        enc[pieces] = dot(ek[h], ev[h], ((0,), (0,))).reshape(PIECES, ROWS, HEAD_DIM)
        so_far = None
        for b in range(blocks):
            rows = pl.ds(b * BLOCK, BLOCK)
            part = dot(dk[h, rows, :], dv[h, rows, :], ((0,), (0,)))
            so_far = part if so_far is None else so_far + part
            if b < blocks - 1:
                cum[h, b] = so_far
        total[pieces] = so_far.reshape(PIECES, ROWS, HEAD_DIM)

    barrier = pltpu.get_barrier_semaphore()
    has = (w > 0, w < wide - 1, z > 0, z < narrow - 1)
    peers = ({"wide": w - 1}, {"wide": w + 1}, {"narrow": z - 1}, {"narrow": z + 1})
    fetch(0)
    for there, peer in zip(has, peers):

        @pl.when(there)
        def _():
            pl.semaphore_signal(barrier, inc=1, device_id=peer, device_id_type=MESH)

    fetch(1)
    fetch(2)
    load_gain.start()

    for there, ref in zip(has, (f_in, g_in, p_in, r_in)):

        @pl.when(jnp.logical_not(there))
        def _():
            ref[...] = jnp.zeros_like(ref)

    states(0)
    load_gain.wait()
    pl.semaphore_wait(barrier, sum(there.astype(jnp.int32) for there in has))

    chains = (
        (f_out, f_in, 0, 1),
        (g_out, g_in, 1, 0),
        (p_out, p_in, 2, 3),
        (r_out, r_in, 3, 2),
    )

    def remote(c, n):
        out, into, _, to = chains[c]
        return pltpu.make_async_remote_copy(
            src_ref=out.at[n],
            dst_ref=into.at[n],
            send_sem=send_sem.at[c, n],
            recv_sem=recv_sem.at[c, n],
            device_id=peers[to],
            device_id_type=MESH,
        )

    def inside(n):
        return jnp.logical_and(n >= 0, n < CHUNKS)

    def link(c, n, value):
        out, into, source, to = chains[c]

        @pl.when(inside(n))
        def _():
            @pl.when(has[source])
            def _():
                remote(c, n).wait_recv()

            @pl.when(has[to])
            def _():
                out[n] = into[n] + value(n)
                remote(c, n).start()

    def make_scores(h):
        load(4, h).wait()
        rows = lax.broadcasted_iota(jnp.int32, (span, span), 0)
        columns = lax.broadcasted_iota(jnp.int32, (span, span), 1)
        keep = jnp.logical_and(rows >= columns, rows // BLOCK == columns // BLOCK)
        for s in range(tokens // span):
            part = pl.ds(s * span, span)
            block = dot(q[h, part, :], dk[h, part, :], ((1,), (1,)))
            block = jnp.where(keep, block, 0.0).astype(jnp.bfloat16)
            for i in range(span // BLOCK):
                near = slice(i * BLOCK, (i + 1) * BLOCK)
                scores[h, pl.ds(s * span + i * BLOCK, BLOCK), :] = block[near, near]

    def finish(h):
        pieces = pl.ds(h * PIECES, PIECES)
        carry = (base[pieces] + p_in[pieces] + r_in[pieces]).reshape(HEAD_DIM, HEAD_DIM)
        columns = pl.ds(pl.multiple_of(h * HEAD_DIM, HEAD_DIM), HEAD_DIM)
        for b in range(blocks):
            rows = pl.ds(b * BLOCK, BLOCK)
            state = carry if b == 0 else carry + cum[h, b - 1]
            left = jnp.concatenate([scores[h, rows, :], q[h, rows, :]], axis=1)
            right = jnp.concatenate([dv[h, rows, :], state.astype(jnp.bfloat16)], axis=0)
            attended = dot(left, right, ((1,), (0,)))
            inverse = lax.rsqrt(jnp.mean(attended * attended, axis=-1, keepdims=True) + 1e-06)
            normed[rows, columns] = (attended * inverse * gain[pl.ds(h, 1), :]).astype(jnp.bfloat16)

    def project(g):
        depth = pl.ds(pl.multiple_of(g * group, group), group)
        load_weight(g).wait()
        tile = min(PROJECT_TILE, out_ref.shape[1])

        def over(store):
            for j in range(out_ref.shape[1] // tile):
                columns = slice(j * tile, (j + 1) * tile)
                store(columns, dot(normed[:, depth], weight[depth, columns], ((1,), (0,))))

        @pl.when(g == 0)
        def _():
            def store(columns, value):
                acc[:, columns] = value

            over(store)

        @pl.when(jnp.logical_and(g > 0, g < GROUPS - 1))
        def _():
            def store(columns, value):
                acc[:, columns] += value

            over(store)

        @pl.when(g == GROUPS - 1)
        def _():
            def store(columns, value):
                out_ref[:, columns] = (acc[:, columns] + value).astype(jnp.bfloat16)

            over(store)

    ready = WIDE_LAG * jnp.maximum(w, wide - 1 - w)
    last = ready + NARROW_LAG * jnp.maximum(z, narrow - 1 - z)

    def slot(t, _):
        h = t // PIECES
        live = jnp.logical_and(h < HEADS, t % PIECES == 0)

        @pl.when(jnp.logical_and(live, h > 0))
        def _():
            states(h)

        link(0, t - WIDE_LAG * w, lambda n: enc[n] + total[n])
        link(1, t - WIDE_LAG * (wide - 1 - w), lambda n: enc[n])

        @pl.when(inside(t - ready))
        def _():
            n = t - ready
            base[n] = enc[n] + f_in[n] + g_in[n]

        link(2, t - ready - NARROW_LAG * z, lambda n: base[n] + total[n])
        link(3, t - ready - NARROW_LAG * (narrow - 1 - z), lambda n: base[n])

        @pl.when(live)
        def _():
            @pl.when(h + 3 < HEADS)
            def _():
                fetch(h + 3)

        after = t - jnp.maximum(last - SCORES_AHEAD, 0) - (PIECES - 1)

        @pl.when(jnp.logical_and(after >= 0, jnp.logical_and(after // PIECES < HEADS, after % PIECES == 0)))
        def _():
            make_scores(after // PIECES)

        early = t // (GROUP * PIECES)

        @pl.when(jnp.logical_and(early < GROUPS, t % (GROUP * PIECES) == 0))
        def _():
            load_weight(early).start()

        n = t - last
        done = n - (PIECES - 1)

        @pl.when(jnp.logical_and(done >= 0, jnp.logical_and(done // PIECES < HEADS, done % PIECES == 0)))
        def _():
            finish(done // PIECES)

        whole = n - (GROUP * PIECES - 1)

        @pl.when(
            jnp.logical_and(
                whole >= 0, jnp.logical_and(whole < CHUNKS, whole % (GROUP * PIECES) == 0)
            )
        )
        def _():
            project(whole // (GROUP * PIECES))

        return 0

    slots = CHUNKS + WIDE_LAG * (wide - 1) + NARROW_LAG * (narrow - 1)
    lax.fori_loop(0, slots, slot, 0)

    for c in range(4):

        @pl.when(has[chains[c][3]])
        def _():
            for n in range(CHUNKS):
                remote(c, n).wait_send()


def local(wide, narrow, dec_queries, dec_keys, dec_values, enc_keys, enc_values, out_weight, head_gain):
    tokens = dec_queries.shape[0]
    blocks = tokens // BLOCK
    depth, model = out_weight.shape
    heads_in = pltpu.VMEM((HEADS, tokens, HEAD_DIM), jnp.bfloat16)
    state = pltpu.VMEM((CHUNKS, ROWS, HEAD_DIM), jnp.float32)
    held = [
        pltpu.with_memory_space_constraint(x, pltpu.HBM)
        for x in (dec_queries, dec_keys, dec_values, enc_keys, enc_values, out_weight)
    ]
    gain = pltpu.with_memory_space_constraint(head_gain.reshape(HEADS, HEAD_DIM), pltpu.HBM)
    return pl.pallas_call(
        functools.partial(kernel, wide, narrow),
        out_shape=jax.ShapeDtypeStruct((tokens, model), jnp.bfloat16),
        in_specs=[pl.BlockSpec(memory_space=pltpu.HBM)] * 7,
        out_specs=pl.BlockSpec(memory_space=pltpu.VMEM),
        scratch_shapes=[heads_in] * 5
        + [
            pltpu.VMEM((depth, model), jnp.bfloat16),
            pltpu.VMEM((HEADS, HEAD_DIM), jnp.float32),
            pltpu.VMEM((HEADS, tokens, BLOCK), jnp.bfloat16),
            pltpu.VMEM((tokens, depth), jnp.bfloat16),
            pltpu.VMEM((tokens, model), jnp.float32),
            state,
            state,
            pltpu.VMEM((HEADS, max(blocks - 1, 1), HEAD_DIM, HEAD_DIM), jnp.float32),
            state,
        ]
        + [state] * 8
        + [
            pltpu.SemaphoreType.DMA((5, HEADS)),
            pltpu.SemaphoreType.DMA((GROUPS,)),
            pltpu.SemaphoreType.DMA,
            pltpu.SemaphoreType.DMA((4, CHUNKS)),
            pltpu.SemaphoreType.DMA((4, CHUNKS)),
        ],
        compiler_params=pltpu.CompilerParams(
            collective_id=0, has_side_effects=True, vmem_limit_bytes=48 * 1024 * 1024
        ),
    )(*held, gain)


def solution(mesh):
    tokens = P(("books", "wide", "narrow"), None)
    return jax.shard_map(
        functools.partial(local, mesh.shape["wide"], mesh.shape["narrow"]),
        mesh=mesh,
        in_specs=(tokens,) * 5 + (P(), P()),
        out_specs=tokens,
        check_vma=False,
    )
```

```python
import functools

import jax
import jax.numpy as jnp
from jax import lax
from jax.experimental import pallas as pl
from jax.experimental.pallas import tpu as pltpu
from jax.sharding import PartitionSpec as P

HEADS = 8
HEAD_DIM = 128
BLOCK = 128
PIECES = 1
ROWS = HEAD_DIM // PIECES
CHUNKS = HEADS * PIECES
GROUP = 2
GROUPS = HEADS // GROUP
NEAR_LAG = 1
FAR_LAG = 3
NARROW_LAG = 3
PROJECT_TILE = 512
SCORES_AHEAD = 3
MESH = pl.DeviceIdType.MESH


def dot(a, b, contract):
    return lax.dot_general(a, b, (contract, ((), ())), preferred_element_type=jnp.float32)


def kernel(
    wide, narrow,
    q_hbm, dk_hbm, dv_hbm, ek_hbm, ev_hbm, weight_hbm, gain_hbm, out_ref,
    q, dk, dv, ek, ev, weight, gain, scores, normed, acc, enc, total, cum, base,
    f_out, g_out, p_out, r_out, f_in, g_in, p_in, r_in,
    load_sem, weight_sem, gain_sem, send_sem, recv_sem,
):
    w = lax.axis_index("wide")
    z = lax.axis_index("narrow")
    tokens = q.shape[1]
    blocks = tokens // BLOCK
    span = 2 * BLOCK if blocks % 2 == 0 else BLOCK
    group = GROUP * HEAD_DIM

    def load(i, h):
        src, dst = ((ek_hbm, ek), (ev_hbm, ev), (dk_hbm, dk), (dv_hbm, dv), (q_hbm, q))[i]
        columns = pl.ds(pl.multiple_of(h * HEAD_DIM, HEAD_DIM), HEAD_DIM)
        return pltpu.make_async_copy(src.at[:, columns], dst.at[h], load_sem.at[i, h])

    def load_weight(g):
        rows = pl.ds(pl.multiple_of(g * group, group), group)
        return pltpu.make_async_copy(weight_hbm.at[rows, :], weight.at[rows, :], weight_sem.at[g])

    load_gain = pltpu.make_async_copy(gain_hbm, gain, gain_sem)

    def fetch(h):
        for i in range(5):
            load(i, h).start()

    def states(h):
        for i in range(4):
            load(i, h).wait()
        pieces = pl.ds(h * PIECES, PIECES)
        enc[pieces] = dot(ek[h], ev[h], ((0,), (0,))).reshape(PIECES, ROWS, HEAD_DIM)
        so_far = None
        for b in range(blocks):
            rows = pl.ds(b * BLOCK, BLOCK)
            part = dot(dk[h, rows, :], dv[h, rows, :], ((0,), (0,)))
            so_far = part if so_far is None else so_far + part
            if b < blocks - 1:
                cum[h, b] = so_far
        total[pieces] = so_far.reshape(PIECES, ROWS, HEAD_DIM)

    barrier = pltpu.get_barrier_semaphore()
    has = (w > 0, w < wide - 1, z > 0, z < narrow - 1)
    peers = ({"wide": w - 1}, {"wide": w + 1}, {"narrow": z - 1}, {"narrow": z + 1})
    fetch(0)
    for there, peer in zip(has, peers):

        @pl.when(there)
        def _():
            pl.semaphore_signal(barrier, inc=1, device_id=peer, device_id_type=MESH)

    fetch(1)
    fetch(2)
    load_gain.start()

    for there, ref in zip(has, (f_in, g_in, p_in, r_in)):

        @pl.when(jnp.logical_not(there))
        def _():
            ref[...] = jnp.zeros_like(ref)

    states(0)
    load_gain.wait()
    pl.semaphore_wait(barrier, sum(there.astype(jnp.int32) for there in has))

    chains = (
        (f_out, f_in, 0, 1),
        (g_out, g_in, 1, 0),
        (p_out, p_in, 2, 3),
        (r_out, r_in, 3, 2),
    )

    def remote(c, n):
        out, into, _, to = chains[c]
        return pltpu.make_async_remote_copy(
            src_ref=out.at[n],
            dst_ref=into.at[n],
            send_sem=send_sem.at[c, n],
            recv_sem=recv_sem.at[c, n],
            device_id=peers[to],
            device_id_type=MESH,
        )

    def inside(n):
        return jnp.logical_and(n >= 0, n < CHUNKS)

    def link(c, n, value):
        out, into, source, to = chains[c]

        @pl.when(inside(n))
        def _():
            @pl.when(has[source])
            def _():
                remote(c, n).wait_recv()

            @pl.when(has[to])
            def _():
                out[n] = into[n] + value(n)
                remote(c, n).start()

    def make_scores(h):
        load(4, h).wait()
        rows = lax.broadcasted_iota(jnp.int32, (span, span), 0)
        columns = lax.broadcasted_iota(jnp.int32, (span, span), 1)
        keep = jnp.logical_and(rows >= columns, rows // BLOCK == columns // BLOCK)
        for s in range(tokens // span):
            part = pl.ds(s * span, span)
            block = dot(q[h, part, :], dk[h, part, :], ((1,), (1,)))
            block = jnp.where(keep, block, 0.0).astype(jnp.bfloat16)
            for i in range(span // BLOCK):
                near = slice(i * BLOCK, (i + 1) * BLOCK)
                scores[h, pl.ds(s * span + i * BLOCK, BLOCK), :] = block[near, near]

    def finish(h):
        pieces = pl.ds(h * PIECES, PIECES)
        carry = (base[pieces] + p_in[pieces] + r_in[pieces]).reshape(HEAD_DIM, HEAD_DIM)
        columns = pl.ds(pl.multiple_of(h * HEAD_DIM, HEAD_DIM), HEAD_DIM)
        for b in range(blocks):
            rows = pl.ds(b * BLOCK, BLOCK)
            state = carry if b == 0 else carry + cum[h, b - 1]
            left = jnp.concatenate([scores[h, rows, :], q[h, rows, :]], axis=1)
            right = jnp.concatenate([dv[h, rows, :], state.astype(jnp.bfloat16)], axis=0)
            attended = dot(left, right, ((1,), (0,)))
            inverse = lax.rsqrt(jnp.mean(attended * attended, axis=-1, keepdims=True) + 1e-06)
            normed[rows, columns] = (attended * inverse * gain[pl.ds(h, 1), :]).astype(jnp.bfloat16)

    def project(g):
        depth = pl.ds(pl.multiple_of(g * group, group), group)
        load_weight(g).wait()
        tile = min(PROJECT_TILE, out_ref.shape[1])

        def over(store):
            for j in range(out_ref.shape[1] // tile):
                columns = slice(j * tile, (j + 1) * tile)
                store(columns, dot(normed[:, depth], weight[depth, columns], ((1,), (0,))))

        @pl.when(g == 0)
        def _():
            def store(columns, value):
                acc[:, columns] = value

            over(store)

        @pl.when(jnp.logical_and(g > 0, g < GROUPS - 1))
        def _():
            def store(columns, value):
                acc[:, columns] += value

            over(store)

        @pl.when(g == GROUPS - 1)
        def _():
            def store(columns, value):
                out_ref[:, columns] = (acc[:, columns] + value).astype(jnp.bfloat16)

            over(store)

    def wide_lag(hops):
        return NEAR_LAG * ((hops + 1) // 2) + FAR_LAG * (hops // 2)

    ready = wide_lag(jnp.maximum(w, wide - 1 - w))
    last = ready + NARROW_LAG * jnp.maximum(z, narrow - 1 - z)

    def slot(t, _):
        h = t // PIECES
        live = jnp.logical_and(h < HEADS, t % PIECES == 0)

        @pl.when(jnp.logical_and(live, h > 0))
        def _():
            states(h)

        link(0, t - wide_lag(w), lambda n: enc[n] + total[n])
        link(1, t - wide_lag(wide - 1 - w), lambda n: enc[n])

        @pl.when(inside(t - ready))
        def _():
            n = t - ready
            base[n] = enc[n] + f_in[n] + g_in[n]

        link(2, t - ready - NARROW_LAG * z, lambda n: base[n] + total[n])
        link(3, t - ready - NARROW_LAG * (narrow - 1 - z), lambda n: base[n])

        @pl.when(live)
        def _():
            @pl.when(h + 3 < HEADS)
            def _():
                fetch(h + 3)

        after = t - jnp.maximum(last - SCORES_AHEAD, 0) - (PIECES - 1)

        @pl.when(jnp.logical_and(after >= 0, jnp.logical_and(after // PIECES < HEADS, after % PIECES == 0)))
        def _():
            make_scores(after // PIECES)

        early = t // (GROUP * PIECES)

        @pl.when(jnp.logical_and(early < GROUPS, t % (GROUP * PIECES) == 0))
        def _():
            load_weight(early).start()

        n = t - last
        done = n - (PIECES - 1)

        @pl.when(jnp.logical_and(done >= 0, jnp.logical_and(done // PIECES < HEADS, done % PIECES == 0)))
        def _():
            finish(done // PIECES)

        whole = n - (GROUP * PIECES - 1)

        @pl.when(
            jnp.logical_and(
                whole >= 0, jnp.logical_and(whole < CHUNKS, whole % (GROUP * PIECES) == 0)
            )
        )
        def _():
            project(whole // (GROUP * PIECES))

        return 0

    slots = CHUNKS + NEAR_LAG * (wide // 2) + FAR_LAG * ((wide - 1) // 2) + NARROW_LAG * (narrow - 1)
    lax.fori_loop(0, slots, slot, 0)

    for c in range(4):

        @pl.when(has[chains[c][3]])
        def _():
            for n in range(CHUNKS):
                remote(c, n).wait_send()


def local(wide, narrow, dec_queries, dec_keys, dec_values, enc_keys, enc_values, out_weight, head_gain):
    tokens = dec_queries.shape[0]
    blocks = tokens // BLOCK
    depth, model = out_weight.shape
    heads_in = pltpu.VMEM((HEADS, tokens, HEAD_DIM), jnp.bfloat16)
    state = pltpu.VMEM((CHUNKS, ROWS, HEAD_DIM), jnp.float32)
    held = [
        pltpu.with_memory_space_constraint(x, pltpu.HBM)
        for x in (dec_queries, dec_keys, dec_values, enc_keys, enc_values, out_weight)
    ]
    gain = pltpu.with_memory_space_constraint(head_gain.reshape(HEADS, HEAD_DIM), pltpu.HBM)
    return pl.pallas_call(
        functools.partial(kernel, wide, narrow),
        out_shape=jax.ShapeDtypeStruct((tokens, model), jnp.bfloat16),
        in_specs=[pl.BlockSpec(memory_space=pltpu.HBM)] * 7,
        out_specs=pl.BlockSpec(memory_space=pltpu.VMEM),
        scratch_shapes=[heads_in] * 5
        + [
            pltpu.VMEM((depth, model), jnp.bfloat16),
            pltpu.VMEM((HEADS, HEAD_DIM), jnp.float32),
            pltpu.VMEM((HEADS, tokens, BLOCK), jnp.bfloat16),
            pltpu.VMEM((tokens, depth), jnp.bfloat16),
            pltpu.VMEM((tokens, model), jnp.float32),
            state,
            state,
            pltpu.VMEM((HEADS, max(blocks - 1, 1), HEAD_DIM, HEAD_DIM), jnp.float32),
            state,
        ]
        + [state] * 8
        + [
            pltpu.SemaphoreType.DMA((5, HEADS)),
            pltpu.SemaphoreType.DMA((GROUPS,)),
            pltpu.SemaphoreType.DMA,
            pltpu.SemaphoreType.DMA((4, CHUNKS)),
            pltpu.SemaphoreType.DMA((4, CHUNKS)),
        ],
        compiler_params=pltpu.CompilerParams(
            collective_id=0, has_side_effects=True, vmem_limit_bytes=48 * 1024 * 1024
        ),
    )(*held, gain)


def solution(mesh):
    tokens = P(("books", "wide", "narrow"), None)
    return jax.shard_map(
        functools.partial(local, mesh.shape["wide"], mesh.shape["narrow"]),
        mesh=mesh,
        in_specs=(tokens,) * 5 + (P(), P()),
        out_specs=tokens,
        check_vma=False,
    )
```

```python
import functools

import jax
import jax.numpy as jnp
from jax import lax
from jax.experimental import pallas as pl
from jax.experimental.pallas import tpu as pltpu
from jax.sharding import PartitionSpec as P

HEADS = 8
HEAD_DIM = 128
BLOCK = 128
PIECES = 1
ROWS = HEAD_DIM // PIECES
CHUNKS = HEADS * PIECES
GROUP = 2
GROUPS = HEADS // GROUP
NEAR_LAG = 1
FAR_LAG = 4
NARROW_LAG = 3
PROJECT_TILE = 512
SCORES_AHEAD = 3
MESH = pl.DeviceIdType.MESH


def dot(a, b, contract):
    return lax.dot_general(a, b, (contract, ((), ())), preferred_element_type=jnp.float32)


def kernel(
    wide, narrow,
    q_hbm, dk_hbm, dv_hbm, ek_hbm, ev_hbm, weight_hbm, gain_hbm, out_ref,
    q, dk, dv, ek, ev, weight, gain, scores, normed, acc, enc, total, cum, base,
    f_out, g_out, p_out, r_out, f_in, g_in, p_in, r_in,
    load_sem, weight_sem, gain_sem, send_sem, recv_sem,
):
    w = lax.axis_index("wide")
    z = lax.axis_index("narrow")
    tokens = q.shape[1]
    blocks = tokens // BLOCK
    span = 2 * BLOCK if blocks % 2 == 0 else BLOCK
    group = GROUP * HEAD_DIM

    def load(i, h):
        src, dst = ((ek_hbm, ek), (ev_hbm, ev), (dk_hbm, dk), (dv_hbm, dv), (q_hbm, q))[i]
        columns = pl.ds(pl.multiple_of(h * HEAD_DIM, HEAD_DIM), HEAD_DIM)
        return pltpu.make_async_copy(src.at[:, columns], dst.at[h], load_sem.at[i, h])

    def load_weight(g):
        rows = pl.ds(pl.multiple_of(g * group, group), group)
        return pltpu.make_async_copy(weight_hbm.at[rows, :], weight.at[rows, :], weight_sem.at[g])

    load_gain = pltpu.make_async_copy(gain_hbm, gain, gain_sem)

    def fetch(h):
        for i in range(5):
            load(i, h).start()

    def states(h):
        for i in range(4):
            load(i, h).wait()
        pieces = pl.ds(h * PIECES, PIECES)
        enc[pieces] = dot(ek[h], ev[h], ((0,), (0,))).reshape(PIECES, ROWS, HEAD_DIM)
        so_far = None
        for b in range(blocks):
            rows = pl.ds(b * BLOCK, BLOCK)
            part = dot(dk[h, rows, :], dv[h, rows, :], ((0,), (0,)))
            so_far = part if so_far is None else so_far + part
            if b < blocks - 1:
                cum[h, b] = so_far
        total[pieces] = so_far.reshape(PIECES, ROWS, HEAD_DIM)

    barrier = pltpu.get_barrier_semaphore()
    has = (w > 0, w < wide - 1, z > 0, z < narrow - 1)
    peers = ({"wide": w - 1}, {"wide": w + 1}, {"narrow": z - 1}, {"narrow": z + 1})
    fetch(0)
    for there, peer in zip(has, peers):

        @pl.when(there)
        def _():
            pl.semaphore_signal(barrier, inc=1, device_id=peer, device_id_type=MESH)

    fetch(1)
    fetch(2)
    load_gain.start()

    for there, ref in zip(has, (f_in, g_in, p_in, r_in)):

        @pl.when(jnp.logical_not(there))
        def _():
            ref[...] = jnp.zeros_like(ref)

    states(0)
    load_gain.wait()
    pl.semaphore_wait(barrier, sum(there.astype(jnp.int32) for there in has))

    chains = (
        (f_out, f_in, 0, 1),
        (g_out, g_in, 1, 0),
        (p_out, p_in, 2, 3),
        (r_out, r_in, 3, 2),
    )

    def remote(c, n):
        out, into, _, to = chains[c]
        return pltpu.make_async_remote_copy(
            src_ref=out.at[n],
            dst_ref=into.at[n],
            send_sem=send_sem.at[c, n],
            recv_sem=recv_sem.at[c, n],
            device_id=peers[to],
            device_id_type=MESH,
        )

    def inside(n):
        return jnp.logical_and(n >= 0, n < CHUNKS)

    def link(c, n, value):
        out, into, source, to = chains[c]

        @pl.when(inside(n))
        def _():
            @pl.when(has[source])
            def _():
                remote(c, n).wait_recv()

            @pl.when(has[to])
            def _():
                out[n] = into[n] + value(n)
                remote(c, n).start()

    def make_scores(h):
        load(4, h).wait()
        rows = lax.broadcasted_iota(jnp.int32, (span, span), 0)
        columns = lax.broadcasted_iota(jnp.int32, (span, span), 1)
        keep = jnp.logical_and(rows >= columns, rows // BLOCK == columns // BLOCK)
        for s in range(tokens // span):
            part = pl.ds(s * span, span)
            block = dot(q[h, part, :], dk[h, part, :], ((1,), (1,)))
            block = jnp.where(keep, block, 0.0).astype(jnp.bfloat16)
            for i in range(span // BLOCK):
                near = slice(i * BLOCK, (i + 1) * BLOCK)
                scores[h, pl.ds(s * span + i * BLOCK, BLOCK), :] = block[near, near]

    def finish(h):
        pieces = pl.ds(h * PIECES, PIECES)
        carry = (base[pieces] + p_in[pieces] + r_in[pieces]).reshape(HEAD_DIM, HEAD_DIM)
        columns = pl.ds(pl.multiple_of(h * HEAD_DIM, HEAD_DIM), HEAD_DIM)
        for b in range(blocks):
            rows = pl.ds(b * BLOCK, BLOCK)
            state = carry if b == 0 else carry + cum[h, b - 1]
            left = jnp.concatenate([scores[h, rows, :], q[h, rows, :]], axis=1)
            right = jnp.concatenate([dv[h, rows, :], state.astype(jnp.bfloat16)], axis=0)
            attended = dot(left, right, ((1,), (0,)))
            inverse = lax.rsqrt(jnp.mean(attended * attended, axis=-1, keepdims=True) + 1e-06)
            normed[rows, columns] = (attended * inverse * gain[pl.ds(h, 1), :]).astype(jnp.bfloat16)

    def project(g):
        depth = pl.ds(pl.multiple_of(g * group, group), group)
        load_weight(g).wait()
        tile = min(PROJECT_TILE, out_ref.shape[1])

        def over(store):
            for j in range(out_ref.shape[1] // tile):
                columns = slice(j * tile, (j + 1) * tile)
                store(columns, dot(normed[:, depth], weight[depth, columns], ((1,), (0,))))

        @pl.when(g == 0)
        def _():
            def store(columns, value):
                acc[:, columns] = value

            over(store)

        @pl.when(jnp.logical_and(g > 0, g < GROUPS - 1))
        def _():
            def store(columns, value):
                acc[:, columns] += value

            over(store)

        @pl.when(g == GROUPS - 1)
        def _():
            def store(columns, value):
                out_ref[:, columns] = (acc[:, columns] + value).astype(jnp.bfloat16)

            over(store)

    def wide_lag(hops):
        return NEAR_LAG * ((hops + 1) // 2) + FAR_LAG * (hops // 2)

    ready = wide_lag(jnp.maximum(w, wide - 1 - w))
    last = ready + NARROW_LAG * jnp.maximum(z, narrow - 1 - z)

    def slot(t, _):
        h = t // PIECES
        live = jnp.logical_and(h < HEADS, t % PIECES == 0)

        @pl.when(jnp.logical_and(live, h > 0))
        def _():
            states(h)

        link(0, t - wide_lag(w), lambda n: enc[n] + total[n])
        link(1, t - wide_lag(wide - 1 - w), lambda n: enc[n])

        @pl.when(inside(t - ready))
        def _():
            n = t - ready
            base[n] = enc[n] + f_in[n] + g_in[n]

        link(2, t - ready - NARROW_LAG * z, lambda n: base[n] + total[n])
        link(3, t - ready - NARROW_LAG * (narrow - 1 - z), lambda n: base[n])

        @pl.when(live)
        def _():
            @pl.when(h + 3 < HEADS)
            def _():
                fetch(h + 3)

        after = t - jnp.maximum(last - SCORES_AHEAD, 0) - (PIECES - 1)

        @pl.when(jnp.logical_and(after >= 0, jnp.logical_and(after // PIECES < HEADS, after % PIECES == 0)))
        def _():
            make_scores(after // PIECES)

        early = t // (GROUP * PIECES)

        @pl.when(jnp.logical_and(early < GROUPS, t % (GROUP * PIECES) == 0))
        def _():
            load_weight(early).start()

        n = t - last
        done = n - (PIECES - 1)

        @pl.when(jnp.logical_and(done >= 0, jnp.logical_and(done // PIECES < HEADS, done % PIECES == 0)))
        def _():
            finish(done // PIECES)

        whole = n - (GROUP * PIECES - 1)

        @pl.when(
            jnp.logical_and(
                whole >= 0, jnp.logical_and(whole < CHUNKS, whole % (GROUP * PIECES) == 0)
            )
        )
        def _():
            project(whole // (GROUP * PIECES))

        return 0

    slots = CHUNKS + NEAR_LAG * (wide // 2) + FAR_LAG * ((wide - 1) // 2) + NARROW_LAG * (narrow - 1)
    lax.fori_loop(0, slots, slot, 0)

    for c in range(4):

        @pl.when(has[chains[c][3]])
        def _():
            for n in range(CHUNKS):
                remote(c, n).wait_send()


def local(wide, narrow, dec_queries, dec_keys, dec_values, enc_keys, enc_values, out_weight, head_gain):
    tokens = dec_queries.shape[0]
    blocks = tokens // BLOCK
    depth, model = out_weight.shape
    heads_in = pltpu.VMEM((HEADS, tokens, HEAD_DIM), jnp.bfloat16)
    state = pltpu.VMEM((CHUNKS, ROWS, HEAD_DIM), jnp.float32)
    held = [
        pltpu.with_memory_space_constraint(x, pltpu.HBM)
        for x in (dec_queries, dec_keys, dec_values, enc_keys, enc_values, out_weight)
    ]
    gain = pltpu.with_memory_space_constraint(head_gain.reshape(HEADS, HEAD_DIM), pltpu.HBM)
    return pl.pallas_call(
        functools.partial(kernel, wide, narrow),
        out_shape=jax.ShapeDtypeStruct((tokens, model), jnp.bfloat16),
        in_specs=[pl.BlockSpec(memory_space=pltpu.HBM)] * 7,
        out_specs=pl.BlockSpec(memory_space=pltpu.VMEM),
        scratch_shapes=[heads_in] * 5
        + [
            pltpu.VMEM((depth, model), jnp.bfloat16),
            pltpu.VMEM((HEADS, HEAD_DIM), jnp.float32),
            pltpu.VMEM((HEADS, tokens, BLOCK), jnp.bfloat16),
            pltpu.VMEM((tokens, depth), jnp.bfloat16),
            pltpu.VMEM((tokens, model), jnp.float32),
            state,
            state,
            pltpu.VMEM((HEADS, max(blocks - 1, 1), HEAD_DIM, HEAD_DIM), jnp.float32),
            state,
        ]
        + [state] * 8
        + [
            pltpu.SemaphoreType.DMA((5, HEADS)),
            pltpu.SemaphoreType.DMA((GROUPS,)),
            pltpu.SemaphoreType.DMA,
            pltpu.SemaphoreType.DMA((4, CHUNKS)),
            pltpu.SemaphoreType.DMA((4, CHUNKS)),
        ],
        compiler_params=pltpu.CompilerParams(
            collective_id=0, has_side_effects=True, vmem_limit_bytes=48 * 1024 * 1024
        ),
    )(*held, gain)


def solution(mesh):
    tokens = P(("books", "wide", "narrow"), None)
    return jax.shard_map(
        functools.partial(local, mesh.shape["wide"], mesh.shape["narrow"]),
        mesh=mesh,
        in_specs=(tokens,) * 5 + (P(), P()),
        out_specs=tokens,
        check_vma=False,
    )
```
